32 devices in a mesh: lon: 8 (over z, core), lat: 4 (over y, x).
Axes of the slice: x: 2, y: 2, z: 4, core: 2. Of those that a mesh axis runs over, the one named last changes fastest.
Arguments:
- fine_input: bfloat16 [4, 48, 192, 384], P(None, 'lat', 'lon'), may hold values from -10 to 10
- merge_gain: float32 [1536], replicated, may hold values from 0.5 to 1.5
- merge_bias: float32 [1536], replicated, may hold values from -1.5 to 1.5
- merge_weight: bfloat16 [1536, 768], P('lat'), may hold values from -2 to 2
- coarse_gain: float32 [768], replicated, may hold values from 0.5 to 1.5
- coarse_bias: float32 [768], replicated, may hold values from -1.5 to 1.5
- coarse_qkv: bfloat16 [768, 2304], P('lat'), may hold values from -2 to 2
- coarse_out: bfloat16 [768, 768], P('lat'), may hold values from -0.21875 to 0.21875
Outputs:
- coarse_output: bfloat16 [4, 24, 96, 768], P(None, 'lat', 'lon')
The draws below stay inside these ranges and needn't reach their ends.
All inputs are finite; a program needn't handle non-finite values.
Results may differ from the reference program's by a relative error of at most 0.013.
Values may be sent and summed in bfloat16 or wider, within the bound.
A program may use at most 128 MiB of HBM per device.

```python
import jax
import jax.numpy as jnp
from jax import lax

WIDTH = 384
WIDTH2 = 768
HEADS2 = 24
LEVELS = 4
LAT = 48
LON = 192


def draw_fine_input(key, part):
    noise_key = jax.random.fold_in(key, 11)
    values = jax.random.truncated_normal(noise_key, -6.0, 6.0, (LEVELS, LAT, LON, WIDTH))
    return values.astype(jnp.bfloat16)


def draw_merge_weight(key, part):
    values = jax.random.truncated_normal(jax.random.fold_in(key, 14), -4.0, 4.0, (4 * WIDTH, WIDTH2)) / jnp.sqrt(4.0 * WIDTH)
    return values.astype(jnp.bfloat16)


def draw_coarse_qkv(key, part):
    values = jax.random.truncated_normal(jax.random.fold_in(key, 15), -4.0, 4.0, (WIDTH2, 3 * WIDTH2)) / jnp.sqrt(1.0 * WIDTH2)
    return values.astype(jnp.bfloat16)


def block_levels(rng, extent, shards, least, largest):
    loudness, own = 1.0, jax.random.fold_in(rng, 6)
    for axis_at, shards_of in shards:
        heights = jnp.exp(jax.random.uniform(jax.random.fold_in(own, axis_at), (shards_of,), jnp.float32, least / len(shards), largest / len(shards)))
        loudness = loudness * jnp.repeat(heights, extent[axis_at] // shards_of).reshape([-1 if axis == axis_at else 1 for axis in range(len(extent))])
    return loudness


def scatter_about(key, extent, deviation, most, split=(), kind=jnp.bfloat16):
    loudness = block_levels(key, extent, split, -0.22, 0.18) if split else 1.0
    entries = jax.random.normal(key, extent, jnp.float32) * deviation * loudness
    return jnp.minimum(jnp.maximum(entries, -most), most).astype(kind)


def setup_inputs(seed: int = 0) -> dict:
    key_of = jax.random.split(jax.random.key(seed), 9)
    fine_input = draw_fine_input(jax.random.fold_in(key_of[8], 71), 0)
    merge_gain = jnp.clip(1.0 + 0.1 * jax.random.normal(key_of[1], (4 * WIDTH,), jnp.float32), 0.5, 1.5)
    merge_bias = scatter_about(key_of[2], (4 * WIDTH,), 0.3, 1.5, (), jnp.float32)
    merge_weight = draw_merge_weight(jax.random.fold_in(key_of[8], 71), 0)
    coarse_gain = jnp.clip(1.0 + 0.1 * jax.random.normal(key_of[4], (WIDTH2,), jnp.float32), 0.5, 1.5)
    coarse_bias = scatter_about(key_of[5], (WIDTH2,), 0.3, 1.5, (), jnp.float32)
    coarse_qkv = draw_coarse_qkv(jax.random.fold_in(key_of[8], 71), 0)
    coarse_out = scatter_about(key_of[7], (WIDTH2, WIDTH2), WIDTH2 ** -0.5, 0.21875, ((0, 4),))
    return dict(fine_input=fine_input, merge_gain=merge_gain, merge_bias=merge_bias, merge_weight=merge_weight, coarse_gain=coarse_gain, coarse_bias=coarse_bias, coarse_qkv=coarse_qkv, coarse_out=coarse_out)


EPSILON = 1e-05

def normalize(values, norm_gain, norm_bias):
    average = lax.optimization_barrier(jnp.mean(values, axis=-1, keepdims=True))
    centered = values - average
    spread = lax.optimization_barrier(jnp.mean(centered * centered, axis=-1, keepdims=True))
    return centered * lax.rsqrt(spread + EPSILON) * norm_gain + norm_bias

def group_ids(level_count, row_start, row_count, row_total):
    level_index = (jnp.arange(level_count, dtype=jnp.int32) + 1) % level_count
    row_index = (row_start + jnp.arange(row_count, dtype=jnp.int32) + 3) % row_total
    level_group = jnp.floor_divide(level_index - 1, 2)
    row_group = jnp.floor_divide(row_index - 3, 6)
    return level_group[:, None] * 65536 + row_group[None, :]

def attend(framed, group_grid, qkv_weight, head_count):
    level_count, row_count, col_count, width = framed.shape
    head_depth = width // head_count
    flat_rows = framed.reshape(-1, width)
    projected = jnp.dot(flat_rows, qkv_weight, preferred_element_type=jnp.float32).astype(jnp.bfloat16)
    window_shape = (level_count // 2, 2, row_count // 6, 6, col_count // 12, 12)
    windows = projected.reshape(window_shape + (3, head_count, head_depth))
    windows = windows.transpose(0, 2, 4, 1, 3, 5, 6, 7, 8).reshape(-1, 144, 3, head_count, head_depth)
    key_grid = jnp.broadcast_to(group_grid[:, :, None], (level_count, row_count, col_count))
    key_windows = key_grid.reshape(window_shape).transpose(0, 2, 4, 1, 3, 5).reshape(-1, 144)
    allowed = key_windows[:, :, None] == key_windows[:, None, :]
    queries = windows[:, :, 0].astype(jnp.float32)
    keys_all = windows[:, :, 1].astype(jnp.float32)
    values = windows[:, :, 2].astype(jnp.float32)
    scores = jnp.einsum('wqhd,wkhd->whqk', queries, keys_all) * head_depth ** (-0.5)
    scores = jnp.where(allowed[:, None], scores, -jnp.inf)
    row_peak = lax.optimization_barrier(jnp.max(scores, axis=-1, keepdims=True))
    weights = jnp.exp(scores - row_peak)
    probabilities = (weights / lax.optimization_barrier(jnp.sum(weights, axis=-1, keepdims=True))).astype(jnp.bfloat16)
    context = jnp.einsum('whqk,wkhd->wqhd', probabilities.astype(jnp.float32), values).astype(jnp.bfloat16)
    context = context.reshape(level_count // 2, row_count // 6, col_count // 12, 2, 6, 12, width)
    return context.transpose(0, 3, 1, 4, 2, 5, 6).reshape(level_count, row_count, col_count, width)

def sublayer(inputs, norm_gain, norm_bias, qkv_weight, out_weight, head_count):
    level_count, row_total, col_total, width = inputs.shape
    blocks = row_total // 6
    normed = normalize(inputs.astype(jnp.float32), norm_gain, norm_bias).astype(jnp.bfloat16)
    framed = jnp.roll(normed, (-1, -3, -6), axis=(0, 1, 2))
    slabs = framed.reshape(level_count, blocks, 6, col_total, width).transpose(1, 0, 2, 3, 4)

    def one_slab(pair_items):
        slab_rows, block_index = pair_items
        grid_ids = group_ids(level_count, block_index * 6, 6, row_total)
        return attend(slab_rows, grid_ids, qkv_weight, head_count)
    context = lax.map(one_slab, (slabs, jnp.arange(blocks, dtype=jnp.int32)))
    context = context.transpose(1, 0, 2, 3, 4).reshape(level_count, row_total, col_total, width)
    context = jnp.roll(context, (1, 3, 6), axis=(0, 1, 2))
    in_blocks = inputs.reshape(level_count, blocks, 6, col_total, width).transpose(1, 0, 2, 3, 4)
    context_blocks = context.reshape(level_count, blocks, 6, col_total, width).transpose(1, 0, 2, 3, 4)

    def finish(pair_items):
        part_in, part_context = pair_items
        branch = jnp.dot(part_context.reshape(-1, width), out_weight, preferred_element_type=jnp.float32)
        return (part_in.astype(jnp.float32) + branch.reshape(part_in.shape)).astype(jnp.bfloat16)
    result = lax.map(finish, (in_blocks, context_blocks))
    return result.transpose(1, 0, 2, 3, 4).reshape(inputs.shape)

def merge_patches(fine, norm_gain, norm_bias, weight):
    level_count, row_total, col_total, width = fine.shape
    patches = fine.reshape(level_count, row_total // 2, 2, col_total // 2, 2, width)
    patches = patches.transpose(0, 1, 3, 2, 4, 5).reshape(level_count, row_total // 2, col_total // 2, 4 * width)
    normed = normalize(patches.astype(jnp.float32), norm_gain, norm_bias).astype(jnp.bfloat16)
    merged = jnp.dot(normed.reshape(-1, 4 * width), weight, preferred_element_type=jnp.float32)
    return merged.astype(jnp.bfloat16).reshape(level_count, row_total // 2, col_total // 2, weight.shape[1])

def reference(fine_input, merge_gain, merge_bias, merge_weight, coarse_gain, coarse_bias, coarse_qkv, coarse_out):
    coarse_input = merge_patches(fine_input, merge_gain, merge_bias, merge_weight)
    return sublayer(coarse_input, coarse_gain, coarse_bias, coarse_qkv, coarse_out, HEADS2)
```

```python
import functools

import jax
import jax.numpy as jnp
import numpy as np
from jax import lax
from jax.experimental import pallas as pl
from jax.experimental.pallas import tpu as pltpu
from jax.sharding import PartitionSpec as P

HEADS2 = 24
EPSILON = 1e-05
MESH = pl.DeviceIdType.MESH
BLOCKED = -1e30
SLOTS = 4
PARTS = 6


def swapped(index, bits):
    bit = 1
    while bit <= bits:
        if bits & bit:
            index = index + bit - 2 * bit * ((index // bit) % 2)
        bit *= 2
    return index


def low_bit(k):
    return k & -k


def high_bit(k):
    return 1 << (k.bit_length() - 1)


def hop_of(k, piece):
    return high_bit(k) if piece == 0 else low_bit(k)


def layout_tables(levels, rows, cols):
    half_rows, half_cols = rows // 2, cols // 2
    per_level = rows * cols
    tokens = levels * per_level
    per_slot = tokens // SLOTS
    padded = -(-per_slot // 16) * 16
    gather = np.zeros((4 * per_level, 4 * per_level), np.float32)
    for i in range(2):
        for j in range(2):
            for a in range(rows):
                for b in range(cols):
                    out_row = (2 * i + j) * per_level + a * cols + b
                    gather[out_row, (2 * a + i) * 2 * cols + 2 * b + j] = 1
    to_slots = np.zeros((SLOTS * padded, tokens), np.float32)
    to_window = np.zeros((tokens, SLOTS * padded), np.float32)
    groups = levels // 2
    window = tokens // groups
    part = window // SLOTS
    per_quarter = half_rows * half_cols
    for q in range(SLOTS):
        row_half, col_half = ((1, 1), (1, 0), (0, 1), (0, 0))[q]
        for f in range(levels):
            level = (f + 1) % levels
            for a in range(half_rows):
                for b in range(half_cols):
                    place = q * padded + (f * half_rows + a) * half_cols + b
                    natural = level * per_level + (row_half * half_rows + a) * cols
                    natural += col_half * half_cols + b
                    to_slots[place, natural] = 1
                    target = (f // 2) * window + q * part + (f % 2) * per_quarter
                    to_window[target + a * half_cols + b, place] = 1
    t = np.arange(window)
    row_id = t // (window // 2)
    level_id = (t // per_quarter) % 2
    row_bias = np.where(row_id[:, None] == row_id[None, :], 0.0, BLOCKED)
    level_bias = np.where(level_id[:, None] == level_id[None, :], 0.0, BLOCKED)
    return (
        gather,
        to_slots,
        to_window,
        row_bias.astype(np.float32),
        level_bias.astype(np.float32),
        padded,
    )


def normalize(values, norm_gain, norm_bias):
    average = jnp.mean(values, axis=-1, keepdims=True)
    centered = values - average
    spread = jnp.mean(centered * centered, axis=-1, keepdims=True)
    return centered * lax.rsqrt(spread + EPSILON) * norm_gain + norm_bias


def dot(a, b):
    return jnp.dot(a, b, preferred_element_type=jnp.float32)


def body(
    dims,
    x_ref,
    mg_ref,
    mb_ref,
    cg_ref,
    cb_ref,
    gather_ref,
    slots_ref,
    slots_t_ref,
    window_ref,
    window_t_ref,
    row_bias_ref,
    level_bias_ref,
    wm_in,
    wq_in,
    wo_in,
    out_ref,
    wm,
    wq,
    wo,
    patches,
    patch_normed,
    coarse,
    own_slots,
    frame,
    framed,
    projected,
    context,
    back_slots,
    home,
    bias,
    own_sem,
    lat_send,
    lat_recv,
    z_send,
    z_recv,
    core_send,
    core_recv,
    halo_send,
    halo_recv,
    back_send,
    back_recv,
):
    lat_count, lon_count, padded, levels = dims
    lat, lon = lax.axis_index("lat"), lax.axis_index("lon")
    core = lon % 2
    z_side = (lon // 2) % 2
    sources, weights = (wm_in, wq_in, wo_in), (wm, wq, wo)
    bits = [1 << b for b in range(lat_count.bit_length() - 1)]
    others = sorted(range(1, lat_count), key=lambda k: (bin(k).count("1"), k))
    up, down = (lat + lat_count - 1) % lat_count, (lat + 1) % lat_count
    left, right = (lon + lon_count - 1) % lon_count, (lon + 1) % lon_count
    z_peer, core_peer = swapped(lon, 2), swapped(lon, 1)

    barrier = pltpu.get_barrier_semaphore()
    greeted = [(swapped(lat, b), lon) for b in bits]
    greeted += [(lat, z_peer), (lat, core_peer)]
    greeted += [(up, lon), (down, lon), (lat, left), (lat, right), (up, left), (down, right)]
    for to_lat, to_lon in greeted:
        pl.semaphore_signal(
            barrier, inc=1, device_id={"lat": to_lat, "lon": to_lon}, device_id_type=MESH
        )
    pl.semaphore_wait(barrier, len(greeted))

    def columns(w, core_side, third):
        wide = weights[w].shape[2] // PARTS
        return pl.ds(pl.multiple_of((core_side * 3 + third) * wide, 128), wide)

    def third_of(piece):
        return z_side if piece == 0 else 2

    def remote(src, dst, send, recv, to_lat, to_lon):
        return pltpu.make_async_remote_copy(
            src_ref=src,
            dst_ref=dst,
            send_sem=send,
            recv_sem=recv,
            device_id={"lat": to_lat, "lon": to_lon},
            device_id_type=MESH,
        )

    def lat_copy(w, k, piece):
        hop = hop_of(k, piece)
        origin = swapped(lat, k ^ hop)
        cols = columns(w, core, third_of(piece))
        dst = weights[w].at[origin, :, cols]
        src = sources[w].at[:, cols] if k == hop else dst
        return remote(
            src, dst, lat_send.at[w, k, piece], lat_recv.at[w, k, piece], swapped(lat, hop), lon
        )

    def z_copy(w, k):
        block = weights[w].at[swapped(lat, k), :, columns(w, core, z_side)]
        return remote(block, block, z_send.at[w, k], z_recv.at[w, k], lat, z_peer)

    def core_copy(w, k, place):
        third = (z_side, 2, 1 - z_side)[place]
        block = weights[w].at[swapped(lat, k), :, columns(w, core, third)]
        return remote(
            block, block, core_send.at[w, k, place], core_recv.at[w, k, place], lat, core_peer
        )

    def start_own(w):
        for piece in range(2):
            for b in bits:
                lat_copy(w, b, piece).start()

    def pump_lat(w):
        for piece in range(2):
            for k in others:
                lat_copy(w, k, piece).wait_recv()
                for further in others:
                    if further != k and further ^ hop_of(further, piece) == k:
                        lat_copy(w, further, piece).start()
                if piece == 0:
                    z_copy(w, k).start()
                core_copy(w, k, piece).start()

    def pump_z(w):
        for k in others:
            z_copy(w, k).wait_recv()
            core_copy(w, k, 2).start()

    def finish(w):
        for k in others:
            for place in range(3):
                core_copy(w, k, place).wait_recv()

    def own_copy(w):
        return pltpu.make_async_copy(sources[w], weights[w].at[lat], own_sem.at[w])

    start_own(0)
    for w in range(3):
        own_copy(w).start()

    per_level = patches.shape[0] // levels
    width = x_ref.shape[2]
    for level in range(levels):
        moved = dot(gather_ref[...], x_ref[level])
        for ij in range(4):
            patches[pl.ds(level * per_level, per_level), pl.ds(ij * width, width)] = moved[
                ij * per_level : (ij + 1) * per_level
            ]
    patch_normed[...] = normalize(patches[...], mg_ref[...], mb_ref[...]).astype(jnp.bfloat16)

    last = jnp.where(lat == lat_count - 1, 1.0, 0.0)
    bias[0] = row_bias_ref[...] * last
    bias[1] = jnp.minimum(row_bias_ref[...] * last, level_bias_ref[...])

    pump_lat(0)
    start_own(1)
    pump_z(0)
    for w in range(3):
        own_copy(w).wait()
    finish(0)

    def project(left_value, weight, store):
        count, rows, cols = weight.shape
        step = 256

        def one(i, carry):
            at = pl.ds(pl.multiple_of(i * step, step), step)
            store(at, dot(left_value, weight[:, :, at].reshape(count * rows, step)))
            return carry

        lax.fori_loop(0, cols // step, one, 0)

    def store_coarse(at, value):
        coarse[:, at] = value.astype(jnp.bfloat16)

    project(patch_normed[...], wm, store_coarse)

    normed = normalize(coarse[...].astype(jnp.float32), cg_ref[...], cb_ref[...])
    own_slots[...] = dot(slots_ref[...], normed.astype(jnp.bfloat16)).astype(jnp.bfloat16)

    def halo_copy(q):
        rows = pl.ds(q * padded, padded)
        to_lat, to_lon = ((lat, left), (up, lon), (up, left))[q - 1]
        return remote(
            own_slots.at[rows], frame.at[rows], halo_send.at[q], halo_recv.at[q], to_lat, to_lon
        )

    def back_copy(q):
        rows = pl.ds(q * padded, padded)
        to_lat, to_lon = ((lat, right), (down, lon), (down, right))[q - 1]
        return remote(
            back_slots.at[rows], home.at[rows], back_send.at[q], back_recv.at[q], to_lat, to_lon
        )

    for q in (3, 2, 1):
        halo_copy(q).start()
    frame[pl.ds(0, padded)] = own_slots[pl.ds(0, padded)]
    pump_lat(1)
    start_own(2)
    pump_z(1)
    for q in (1, 2, 3):
        halo_copy(q).wait_recv()
    framed[...] = dot(window_ref[...], frame[...]).astype(jnp.bfloat16)
    finish(1)

    def store_projected(at, value):
        projected[:, at] = value.astype(jnp.bfloat16)

    project(framed[...], wq, store_projected)
    pump_lat(2)
    pump_z(2)

    model = context.shape[1]
    depth = model // HEADS2
    packed = 128 // depth
    window = bias.shape[1]
    scale = depth ** (-0.5)
    lane = lax.broadcasted_iota(jnp.int32, (window, 128), 1)
    masks = [(lane >= h * depth) & (lane < (h + 1) * depth) for h in range(packed)]

    for g in range(levels // 2):
        rows = pl.ds(g * window, window)

        def one_group(i, carry):
            def lanes(which):
                return pl.ds(pl.multiple_of(which * model + i * 128, 128), 128)

            queries = projected[rows, lanes(0)].astype(jnp.float32)
            keys = projected[rows, lanes(1)]
            values = projected[rows, lanes(2)]
            result = jnp.zeros((window, 128), jnp.float32)
            for h in range(packed):
                one_head = jnp.where(masks[h], queries, 0.0).astype(jnp.bfloat16)
                scores = lax.dot_general(
                    one_head, keys, (((1,), (1,)), ((), ())), preferred_element_type=jnp.float32
                )
                scores = scores * scale + bias[g]
                peak = jnp.max(scores, axis=-1, keepdims=True)
                shares = jnp.exp(scores - peak)
                total = jnp.sum(shares, axis=-1, keepdims=True)
                mixed = dot((shares / total).astype(jnp.bfloat16), values)
                result = jnp.where(masks[h], mixed, result)
            context[rows, pl.ds(pl.multiple_of(i * 128, 128), 128)] = result.astype(jnp.bfloat16)
            return carry

        lax.fori_loop(0, model // 128, one_group, 0)

    back_slots[...] = dot(window_t_ref[...], context[...]).astype(jnp.bfloat16)
    for q in (3, 2, 1):
        back_copy(q).start()
    home[pl.ds(0, padded)] = back_slots[pl.ds(0, padded)]
    finish(2)
    for q in (1, 2, 3):
        back_copy(q).wait_recv()
    ordered = dot(slots_t_ref[...], home[...]).astype(jnp.bfloat16)

    def store_out(at, value):
        out_ref[:, at] = (coarse[:, at].astype(jnp.float32) + value).astype(jnp.bfloat16)

    project(ordered, wo, store_out)

    for w in range(3):
        for k in others:
            for piece in range(2):
                lat_copy(w, k, piece).wait_send()
            z_copy(w, k).wait_send()
            for place in range(3):
                core_copy(w, k, place).wait_send()
    for q in (1, 2, 3):
        halo_copy(q).wait_send()
        back_copy(q).wait_send()


def shards(
    fine_input,
    merge_gain,
    merge_bias,
    merge_weight,
    coarse_gain,
    coarse_bias,
    coarse_qkv,
    coarse_out,
):
    lat_count, lon_count = lax.axis_size("lat"), lax.axis_size("lon")
    levels, fine_rows, fine_cols, width = fine_input.shape
    rows, cols = fine_rows // 2, fine_cols // 2
    model = merge_weight.shape[1]
    assert rows == 6 and cols == 12 and levels == 4
    assert lat_count & (lat_count - 1) == 0 and lon_count % 4 == 0
    gather, to_slots, to_window, row_bias, level_bias, padded = layout_tables(levels, rows, cols)
    tokens = levels * rows * cols
    half = jnp.bfloat16
    operands = (
        fine_input.reshape(levels, fine_rows * fine_cols, width),
        merge_gain.reshape(1, -1),
        merge_bias.reshape(1, -1),
        coarse_gain.reshape(1, -1),
        coarse_bias.reshape(1, -1),
        jnp.asarray(gather, half),
        jnp.asarray(to_slots, half),
        jnp.asarray(to_slots.T, half),
        jnp.asarray(to_window, half),
        jnp.asarray(to_window.T, half),
        jnp.asarray(row_bias),
        jnp.asarray(level_bias),
        merge_weight,
        coarse_qkv,
        coarse_out,
    )
    slots = SLOTS * padded
    window = tokens // (levels // 2)
    result = pl.pallas_call(
        functools.partial(body, (lat_count, lon_count, padded, levels)),
        out_shape=jax.ShapeDtypeStruct((tokens, model), half),
        in_specs=[pl.BlockSpec(memory_space=pltpu.VMEM)] * 12
        + [pl.BlockSpec(memory_space=pl.ANY)] * 3,
        out_specs=pl.BlockSpec(memory_space=pltpu.VMEM),
        scratch_shapes=[
            pltpu.VMEM((lat_count,) + merge_weight.shape, half),
            pltpu.VMEM((lat_count,) + coarse_qkv.shape, half),
            pltpu.VMEM((lat_count,) + coarse_out.shape, half),
            pltpu.VMEM((tokens, 4 * width), jnp.float32),
            pltpu.VMEM((tokens, 4 * width), half),
            pltpu.VMEM((tokens, model), half),
            pltpu.VMEM((slots, model), half),
            pltpu.VMEM((slots, model), half),
            pltpu.VMEM((tokens, model), half),
            pltpu.VMEM((tokens, 3 * model), half),
            pltpu.VMEM((tokens, model), half),
            pltpu.VMEM((slots, model), half),
            pltpu.VMEM((slots, model), half),
            pltpu.VMEM((2, window, window), jnp.float32),
            pltpu.SemaphoreType.DMA((3,)),
            pltpu.SemaphoreType.DMA((3, lat_count, 2)),
            pltpu.SemaphoreType.DMA((3, lat_count, 2)),
            pltpu.SemaphoreType.DMA((3, lat_count)),
            pltpu.SemaphoreType.DMA((3, lat_count)),
            pltpu.SemaphoreType.DMA((3, lat_count, 3)),
            pltpu.SemaphoreType.DMA((3, lat_count, 3)),
            pltpu.SemaphoreType.DMA((SLOTS,)),
            pltpu.SemaphoreType.DMA((SLOTS,)),
            pltpu.SemaphoreType.DMA((SLOTS,)),
            pltpu.SemaphoreType.DMA((SLOTS,)),
        ],
        compiler_params=pltpu.CompilerParams(collective_id=0, has_side_effects=True),
    )(*operands)
    return result.reshape(levels, rows, cols, model)


def solution(mesh):
    in_specs = (
        P(None, "lat", "lon", None),
        P(),
        P(),
        P("lat", None),
        P(),
        P(),
        P("lat", None),
        P("lat", None),
    )
    out_specs = P(None, "lat", "lon", None)
    return jax.shard_map(shards, mesh=mesh, in_specs=in_specs, out_specs=out_specs, check_vma=False)
```

```python
import functools

import jax
import jax.numpy as jnp
import numpy as np
from jax import lax
from jax.experimental import pallas as pl
from jax.experimental.pallas import tpu as pltpu
from jax.sharding import PartitionSpec as P

HEADS2 = 24
EPSILON = 1e-05
MESH = pl.DeviceIdType.MESH
BLOCKED = -1e30
SLOTS = 4
PARTS = 6


def swapped(index, bits):
    bit = 1
    while bit <= bits:
        if bits & bit:
            index = index + bit - 2 * bit * ((index // bit) % 2)
        bit *= 2
    return index


def low_bit(k):
    return k & -k


def high_bit(k):
    return 1 << (k.bit_length() - 1)


def hop_of(k, piece):
    return high_bit(k) if piece == 0 else low_bit(k)


def layout_tables(levels, rows, cols):
    half_rows, half_cols = rows // 2, cols // 2
    per_level = rows * cols
    tokens = levels * per_level
    per_slot = tokens // SLOTS
    padded = -(-per_slot // 16) * 16
    gather = np.zeros((4 * per_level, 4 * per_level), np.float32)
    for i in range(2):
        for j in range(2):
            for a in range(rows):
                for b in range(cols):
                    out_row = (2 * i + j) * per_level + a * cols + b
                    gather[out_row, (2 * a + i) * 2 * cols + 2 * b + j] = 1
    to_slots = np.zeros((SLOTS * padded, tokens), np.float32)
    to_window = np.zeros((tokens, SLOTS * padded), np.float32)
    groups = levels // 2
    window = tokens // groups
    part = window // SLOTS
    per_quarter = half_rows * half_cols
    for q in range(SLOTS):
        row_half, col_half = ((1, 1), (1, 0), (0, 1), (0, 0))[q]
        for f in range(levels):
            level = (f + 1) % levels
            for a in range(half_rows):
                for b in range(half_cols):
                    place = q * padded + (f * half_rows + a) * half_cols + b
                    natural = (row_half * half_rows + a) * cols + col_half * half_cols + b
                    to_slots[place, natural * levels + level] = 1
                    target = (f // 2) * window + q * part + (f % 2) * per_quarter
                    to_window[target + a * half_cols + b, place] = 1
    t = np.arange(window)
    row_id = t // (window // 2)
    level_id = (t // per_quarter) % 2
    row_bias = np.where(row_id[:, None] == row_id[None, :], 0.0, BLOCKED)
    level_bias = np.where(level_id[:, None] == level_id[None, :], 0.0, BLOCKED)
    return (
        gather,
        to_slots,
        to_window,
        np.tile(row_bias, (1, 4)).astype(np.float32),
        np.tile(level_bias, (1, 4)).astype(np.float32),
        padded,
    )


def normalize(values, norm_gain, norm_bias):
    average = jnp.mean(values, axis=-1, keepdims=True)
    centered = values - average
    spread = jnp.mean(centered * centered, axis=-1, keepdims=True)
    return centered * lax.rsqrt(spread + EPSILON) * norm_gain + norm_bias


def dot(a, b):
    return jnp.dot(a, b, preferred_element_type=jnp.float32)


def body(
    dims,
    x_in,
    mg_in,
    mb_in,
    cg_in,
    cb_in,
    gather_in,
    slots_in,
    slots_t_in,
    window_in,
    window_t_in,
    row_bias_in,
    level_bias_in,
    wm_in,
    wq_in,
    wo_in,
    out_ref,
    wm,
    wq,
    wo,
    patches,
    patch_normed,
    coarse,
    own_slots,
    frame,
    framed,
    projected,
    context,
    back_slots,
    home,
    bias,
    own_sem,
    lat_send,
    lat_recv,
    z_send,
    z_recv,
    core_send,
    core_recv,
    halo_send,
    halo_recv,
    back_send,
    back_recv,
    fetch_sem,
    x_ref,
    mg_ref,
    mb_ref,
    cg_ref,
    cb_ref,
    gather_ref,
    slots_ref,
    slots_t_ref,
    window_ref,
    window_t_ref,
    row_bias_ref,
    level_bias_ref,
):
    lat_count, lon_count, padded, levels = dims
    lat, lon = lax.axis_index("lat"), lax.axis_index("lon")
    core = lon % 2
    z_side = (lon // 2) % 2
    sources, weights = (wm_in, wq_in, wo_in), (wm, wq, wo)
    bits = [1 << b for b in range(lat_count.bit_length() - 1)]
    others = sorted(range(1, lat_count), key=lambda k: (bin(k).count("1"), k))
    up, down = (lat + lat_count - 1) % lat_count, (lat + 1) % lat_count
    left, right = (lon + lon_count - 1) % lon_count, (lon + 1) % lon_count
    z_peer, core_peer = swapped(lon, 2), swapped(lon, 1)

    barrier = pltpu.get_barrier_semaphore()
    greeted = [(swapped(lat, b), lon) for b in bits]
    greeted += [(lat, z_peer), (lat, core_peer)]
    greeted += [(up, lon), (down, lon), (lat, left), (lat, right), (up, left), (down, right)]
    for to_lat, to_lon in greeted:
        pl.semaphore_signal(
            barrier, inc=1, device_id={"lat": to_lat, "lon": to_lon}, device_id_type=MESH
        )
    outside = (
        x_in,
        mg_in,
        mb_in,
        cg_in,
        cb_in,
        gather_in,
        slots_in,
        slots_t_in,
        window_in,
        window_t_in,
        row_bias_in,
        level_bias_in,
    )
    inside = (
        x_ref,
        mg_ref,
        mb_ref,
        cg_ref,
        cb_ref,
        gather_ref,
        slots_ref,
        slots_t_ref,
        window_ref,
        window_t_ref,
        row_bias_ref,
        level_bias_ref,
    )
    fetches = [
        pltpu.make_async_copy(outside[i], inside[i], fetch_sem.at[i]) for i in range(len(inside))
    ]
    for i in (0, 5, 1, 2, 3, 4, 6, 8, 10, 11, 7, 9):
        fetches[i].start()
    pl.semaphore_wait(barrier, len(greeted))

    def part_rows(w, core_side, third):
        tall = weights[w].shape[1] // PARTS
        return pl.ds(pl.multiple_of((core_side * 3 + third) * tall, tall), tall)

    def third_of(piece):
        return z_side if piece == 0 else 2

    def remote(src, dst, send, recv, to_lat, to_lon):
        return pltpu.make_async_remote_copy(
            src_ref=src,
            dst_ref=dst,
            send_sem=send,
            recv_sem=recv,
            device_id={"lat": to_lat, "lon": to_lon},
            device_id_type=MESH,
        )

    def lat_copy(w, k, piece):
        hop = hop_of(k, piece)
        origin = swapped(lat, k ^ hop)
        rows = part_rows(w, core, third_of(piece))
        dst = weights[w].at[origin, rows]
        src = sources[w].at[rows] if k == hop else dst
        return remote(
            src, dst, lat_send.at[w, k, piece], lat_recv.at[w, k, piece], swapped(lat, hop), lon
        )

    def z_copy(w, k):
        block = weights[w].at[swapped(lat, k), part_rows(w, core, z_side)]
        return remote(block, block, z_send.at[w, k], z_recv.at[w, k], lat, z_peer)

    def core_copy(w, k, place):
        third = (z_side, 2, 1 - z_side)[place]
        block = weights[w].at[swapped(lat, k), part_rows(w, core, third)]
        return remote(
            block, block, core_send.at[w, k, place], core_recv.at[w, k, place], lat, core_peer
        )

    def start_own(w):
        for step in range(2):
            for at, b in enumerate(bits):
                lat_copy(w, b, (step + at) % 2).start()

    arrivals = [(k, piece) for k in others for piece in range(2)]
    arrivals.sort(key=lambda a: (bin(a[0]).count("1"), (bits.index(hop_of(*a)) + a[1]) % 2))
    firsts = [a for a in arrivals if a[0] in bits]
    rest = [a for a in arrivals if a[0] not in bits]

    def pump(w, which):
        for k, piece in which:
            lat_copy(w, k, piece).wait_recv()
            for further in others:
                if further != k and further ^ hop_of(further, piece) == k:
                    lat_copy(w, further, piece).start()
            if piece == 0:
                z_copy(w, k).start()
            core_copy(w, k, piece).start()

    def pump_z(w):
        for k in others:
            z_copy(w, k).wait_recv()
            core_copy(w, k, 2).start()

    def finish(w):
        for k in others:
            for place in range(3):
                core_copy(w, k, place).wait_recv()

    def own_copy(w):
        return pltpu.make_async_copy(sources[w], weights[w].at[lat], own_sem.at[w])

    start_own(0)
    for w in range(3):
        own_copy(w).start()

    per_level = patches.shape[1] // levels
    width = x_ref.shape[2]
    fetches[0].wait()
    fetches[5].wait()
    for level in range(levels):
        moved = dot(gather_ref[...], x_ref[level])
        for ij in range(4):
            for at in range(0, width, 128):
                patches[
                    (ij * width + at) // 128, pl.ds(level, per_level, stride=levels), :
                ] = moved[ij * per_level : (ij + 1) * per_level, at : at + 128]
    pump(0, firsts)
    start_own(1)
    fetches[1].wait()
    fetches[2].wait()
    whole = jnp.concatenate([patches[b] for b in range(patches.shape[0])], axis=1)
    patch_normed[...] = normalize(whole, mg_ref[...][None], mb_ref[...][None]).astype(
        jnp.bfloat16
    )
    pump(0, rest)
    for i in (3, 4, 6, 7, 8, 9, 10, 11):
        fetches[i].wait()
    last = jnp.where(lat == lat_count - 1, 1.0, 0.0)
    bias[0] = row_bias_ref[...] * last
    bias[1] = jnp.minimum(row_bias_ref[...] * last, level_bias_ref[...])
    pump_z(0)
    for w in range(3):
        own_copy(w).wait()
    finish(0)

    def project(left_value, weight, store):
        count, rows, cols = weight.shape
        step = 256

        def one(i, carry):
            at = pl.ds(pl.multiple_of(i * step, step), step)
            store(at, dot(left_value, weight[:, :, at].reshape(count * rows, step)))
            return carry

        lax.fori_loop(0, cols // step, one, 0)

    def store_coarse(at, value):
        coarse[:, at] = value.astype(jnp.bfloat16)

    project(patch_normed[...], wm, store_coarse)

    pump(1, firsts)
    normed = normalize(coarse[...].astype(jnp.float32), cg_ref[...][None], cb_ref[...][None])
    own_slots[...] = dot(slots_ref[...], normed.astype(jnp.bfloat16)).astype(jnp.bfloat16)

    model = context.shape[1]
    split = model // 2

    def halo_copy(q):
        rows = pl.ds(q * padded, padded)
        to_lat, to_lon = ((lat, left), (up, lon), (up, left))[q - 1]
        return remote(
            own_slots.at[rows], frame.at[rows], halo_send.at[q], halo_recv.at[q], to_lat, to_lon
        )

    def back_copy(q, half):
        rows, lanes = pl.ds(q * padded, padded), pl.ds(half * split, split)
        to_lat, to_lon = ((lat, right), (down, lon), (down, right))[q - 1]
        return remote(
            back_slots.at[rows, lanes],
            home.at[rows, lanes],
            back_send.at[q, half],
            back_recv.at[q, half],
            to_lat,
            to_lon,
        )

    for q in (3, 2, 1):
        halo_copy(q).start()
    frame[pl.ds(0, padded)] = own_slots[pl.ds(0, padded)]
    start_own(2)
    pump(1, rest)
    pump_z(1)
    for q in (1, 2, 3):
        halo_copy(q).wait_recv()
    framed[...] = dot(window_ref[...], frame[...]).astype(jnp.bfloat16)
    finish(1)

    def store_projected(at, value):
        projected[:, at] = value.astype(jnp.bfloat16)

    project(framed[...], wq, store_projected)
    pump(2, firsts)

    depth = model // HEADS2
    packed = 128 // depth
    window = bias.shape[1]
    scale = depth ** (-0.5)
    lane = lax.broadcasted_iota(jnp.int32, (window, 128), 1)
    masks = [(lane >= h * depth) & (lane < (h + 1) * depth) for h in range(packed)]

    for half in range(2):
        for g in range(levels // 2):
            rows = pl.ds(g * window, window)

            def one_group(i, carry):
                def lanes(which):
                    return pl.ds(pl.multiple_of(which * model + i * 128, 128), 128)

                queries = projected[rows, lanes(0)]
                keys = projected[rows, lanes(1)]
                values = projected[rows, lanes(2)]
                nothing = jnp.zeros_like(queries)
                stacked = jnp.concatenate([jnp.where(m, queries, nothing) for m in masks], axis=0)
                scores = lax.dot_general(
                    keys, stacked, (((1,), (1,)), ((), ())), preferred_element_type=jnp.float32
                )
                scores = scores * scale + bias[g]
                peak = jnp.max(scores, axis=0, keepdims=True)
                shares = jnp.exp(scores - peak)
                total = jnp.sum(shares, axis=0, keepdims=True)
                probs = (shares * (1.0 / total)).astype(jnp.bfloat16)
                mixed = lax.dot_general(
                    probs, values, (((0,), (0,)), ((), ())), preferred_element_type=jnp.float32
                )
                result = mixed[:window]
                for h in range(1, packed):
                    result = jnp.where(masks[h], mixed[h * window : (h + 1) * window], result)
                at = pl.ds(pl.multiple_of(i * 128, 128), 128)
                context[rows, at] = result.astype(jnp.bfloat16)
                return carry

            lax.fori_loop(half * split // 128, (half + 1) * split // 128, one_group, 0)
        lanes_of = pl.ds(half * split, split)
        back_slots[:, lanes_of] = dot(window_t_ref[...], context[:, lanes_of]).astype(jnp.bfloat16)
        for q in (3, 2, 1):
            back_copy(q, half).start()
        home[pl.ds(0, padded), lanes_of] = back_slots[pl.ds(0, padded), lanes_of]
        if half == 0:
            pump(2, rest)
            pump_z(2)
    finish(2)
    for q in (1, 2, 3):
        for half in range(2):
            back_copy(q, half).wait_recv()
    ordered = dot(slots_t_ref[...], home[...]).astype(jnp.bfloat16)

    def store_out(at, value):
        out_ref[:, at] = (coarse[:, at].astype(jnp.float32) + value).astype(jnp.bfloat16)

    project(ordered, wo, store_out)

    for w in range(3):
        for k in others:
            for piece in range(2):
                lat_copy(w, k, piece).wait_send()
            z_copy(w, k).wait_send()
            for place in range(3):
                core_copy(w, k, place).wait_send()
    for q in (1, 2, 3):
        halo_copy(q).wait_send()
        for half in range(2):
            back_copy(q, half).wait_send()


def shards(
    fine_input,
    merge_gain,
    merge_bias,
    merge_weight,
    coarse_gain,
    coarse_bias,
    coarse_qkv,
    coarse_out,
):
    lat_count, lon_count = lax.axis_size("lat"), lax.axis_size("lon")
    levels, fine_rows, fine_cols, width = fine_input.shape
    rows, cols = fine_rows // 2, fine_cols // 2
    model = merge_weight.shape[1]
    assert rows == 6 and cols == 12 and levels == 4
    assert lat_count & (lat_count - 1) == 0 and lon_count % 4 == 0
    gather, to_slots, to_window, row_bias, level_bias, padded = layout_tables(levels, rows, cols)
    tokens = levels * rows * cols
    half = jnp.bfloat16
    operands = (
        fine_input.reshape(levels, fine_rows * fine_cols, width),
        merge_gain,
        merge_bias,
        coarse_gain,
        coarse_bias,
        jnp.asarray(gather, half),
        jnp.asarray(to_slots, half),
        jnp.asarray(to_slots.T, half),
        jnp.asarray(to_window, half),
        jnp.asarray(to_window.T, half),
        jnp.asarray(row_bias),
        jnp.asarray(level_bias),
        merge_weight,
        coarse_qkv,
        coarse_out,
    )
    slots = SLOTS * padded
    window = tokens // (levels // 2)
    result = pl.pallas_call(
        functools.partial(body, (lat_count, lon_count, padded, levels)),
        out_shape=jax.ShapeDtypeStruct((tokens, model), half),
        in_specs=[pl.BlockSpec(memory_space=pl.ANY)] * len(operands),
        out_specs=pl.BlockSpec(memory_space=pltpu.VMEM),
        scratch_shapes=[
            pltpu.VMEM((lat_count,) + merge_weight.shape, half),
            pltpu.VMEM((lat_count,) + coarse_qkv.shape, half),
            pltpu.VMEM((lat_count,) + coarse_out.shape, half),
            pltpu.VMEM((4 * width // 128, tokens, 128), jnp.float32),
            pltpu.VMEM((tokens, 4 * width), half),
            pltpu.VMEM((tokens, model), half),
            pltpu.VMEM((slots, model), half),
            pltpu.VMEM((slots, model), half),
            pltpu.VMEM((tokens, model), half),
            pltpu.VMEM((tokens, 3 * model), half),
            pltpu.VMEM((tokens, model), half),
            pltpu.VMEM((slots, model), half),
            pltpu.VMEM((slots, model), half),
            pltpu.VMEM((2, window, 4 * window), jnp.float32),
            pltpu.SemaphoreType.DMA((3,)),
            pltpu.SemaphoreType.DMA((3, lat_count, 2)),
            pltpu.SemaphoreType.DMA((3, lat_count, 2)),
            pltpu.SemaphoreType.DMA((3, lat_count)),
            pltpu.SemaphoreType.DMA((3, lat_count)),
            pltpu.SemaphoreType.DMA((3, lat_count, 3)),
            pltpu.SemaphoreType.DMA((3, lat_count, 3)),
            pltpu.SemaphoreType.DMA((SLOTS,)),
            pltpu.SemaphoreType.DMA((SLOTS,)),
            pltpu.SemaphoreType.DMA((SLOTS, 2)),
            pltpu.SemaphoreType.DMA((SLOTS, 2)),
            pltpu.SemaphoreType.DMA((len(operands) - 3,)),
        ]
        + [pltpu.VMEM(operand.shape, operand.dtype) for operand in operands[:-3]],
        compiler_params=pltpu.CompilerParams(collective_id=0, has_side_effects=True),
    )(*operands)
    return result.reshape(rows, cols, levels, model).transpose(2, 0, 1, 3)


def solution(mesh):
    in_specs = (
        P(None, "lat", "lon", None),
        P(),
        P(),
        P("lat", None),
        P(),
        P(),
        P("lat", None),
        P("lat", None),
    )
    out_specs = P(None, "lat", "lon", None)
    return jax.shard_map(shards, mesh=mesh, in_specs=in_specs, out_specs=out_specs, check_vma=False)
```

```python
import functools

import jax
import jax.numpy as jnp
import numpy as np
from jax import lax
from jax.experimental import pallas as pl
from jax.experimental.pallas import tpu as pltpu
from jax.sharding import PartitionSpec as P

HEADS2 = 24
EPSILON = 1e-05
MESH = pl.DeviceIdType.MESH
BLOCKED = -1e30
SLOTS = 4
BACK_PARTS = 3
PARTS = 6


def swapped(index, bits):
    bit = 1
    while bit <= bits:
        if bits & bit:
            index = index + bit - 2 * bit * ((index // bit) % 2)
        bit *= 2
    return index


def low_bit(k):
    return k & -k


def high_bit(k):
    return 1 << (k.bit_length() - 1)


def hop_of(k, piece):
    return high_bit(k) if piece == 0 else low_bit(k)


def layout_tables(levels, rows, cols):
    half_rows, half_cols = rows // 2, cols // 2
    per_level = rows * cols
    tokens = levels * per_level
    per_slot = tokens // SLOTS
    padded = -(-per_slot // 16) * 16
    gather = np.zeros((4 * per_level, 4 * per_level), np.float32)
    for i in range(2):
        for j in range(2):
            for a in range(rows):
                for b in range(cols):
                    out_row = (2 * i + j) * per_level + a * cols + b
                    gather[out_row, (2 * a + i) * 2 * cols + 2 * b + j] = 1
    to_slots = np.zeros((SLOTS * padded, tokens), np.float32)
    to_window = np.zeros((tokens, SLOTS * padded), np.float32)
    groups = levels // 2
    window = tokens // groups
    part = window // SLOTS
    per_quarter = half_rows * half_cols
    for q in range(SLOTS):
        row_half, col_half = ((1, 1), (1, 0), (0, 1), (0, 0))[q]
        for f in range(levels):
            level = (f + 1) % levels
            for a in range(half_rows):
                for b in range(half_cols):
                    place = q * padded + (f * half_rows + a) * half_cols + b
                    natural = (row_half * half_rows + a) * cols + col_half * half_cols + b
                    to_slots[place, natural * levels + level] = 1
                    target = (f // 2) * window + q * part + (f % 2) * per_quarter
                    to_window[target + a * half_cols + b, place] = 1
    t = np.arange(window)
    row_id = t // (window // 2)
    level_id = (t // per_quarter) % 2
    row_bias = np.where(row_id[:, None] == row_id[None, :], 0.0, BLOCKED)
    level_bias = np.where(level_id[:, None] == level_id[None, :], 0.0, BLOCKED)
    return (
        gather,
        to_slots,
        to_window,
        np.tile(row_bias, (1, 4)).astype(np.float32),
        np.tile(level_bias, (1, 4)).astype(np.float32),
        padded,
    )


def normalize(values, norm_gain, norm_bias):
    average = jnp.mean(values, axis=-1, keepdims=True)
    centered = values - average
    spread = jnp.mean(centered * centered, axis=-1, keepdims=True)
    return centered * lax.rsqrt(spread + EPSILON) * norm_gain + norm_bias


def dot(a, b):
    return jnp.dot(a, b, preferred_element_type=jnp.float32)


def body(
    dims,
    x_in,
    mg_in,
    mb_in,
    cg_in,
    cb_in,
    gather_in,
    slots_in,
    slots_t_in,
    window_in,
    window_t_in,
    row_bias_in,
    level_bias_in,
    wm_in,
    wq_in,
    wo_in,
    out_ref,
    wm,
    wq,
    wo,
    patches,
    patch_normed,
    coarse,
    own_slots,
    frame,
    framed,
    projected,
    context,
    back_slots,
    home,
    bias,
    own_sem,
    lat_send,
    lat_recv,
    z_send,
    z_recv,
    core_send,
    core_recv,
    halo_send,
    halo_recv,
    back_send,
    back_recv,
    fetch_sem,
    x_ref,
    mg_ref,
    mb_ref,
    cg_ref,
    cb_ref,
    gather_ref,
    slots_ref,
    slots_t_ref,
    window_ref,
    window_t_ref,
    row_bias_ref,
    level_bias_ref,
):
    lat_count, lon_count, padded, levels = dims
    lat, lon = lax.axis_index("lat"), lax.axis_index("lon")
    core = lon % 2
    z_side = (lon // 2) % 2
    sources, weights = (wm_in, wq_in, wo_in), (wm, wq, wo)
    bits = [1 << b for b in range(lat_count.bit_length() - 1)]
    others = sorted(range(1, lat_count), key=lambda k: (bin(k).count("1"), k))
    up, down = (lat + lat_count - 1) % lat_count, (lat + 1) % lat_count
    left, right = (lon + lon_count - 1) % lon_count, (lon + 1) % lon_count
    z_peer, core_peer = swapped(lon, 2), swapped(lon, 1)

    barrier = pltpu.get_barrier_semaphore()
    greeted = [(swapped(lat, b), lon) for b in bits]
    greeted += [(lat, z_peer), (lat, core_peer)]
    greeted += [(up, lon), (down, lon), (lat, left), (lat, right), (up, left), (down, right)]
    for to_lat, to_lon in greeted:
        pl.semaphore_signal(
            barrier, inc=1, device_id={"lat": to_lat, "lon": to_lon}, device_id_type=MESH
        )
    outside = (
        x_in,
        mg_in,
        mb_in,
        cg_in,
        cb_in,
        gather_in,
        slots_in,
        slots_t_in,
        window_in,
        window_t_in,
        row_bias_in,
        level_bias_in,
    )
    inside = (
        x_ref,
        mg_ref,
        mb_ref,
        cg_ref,
        cb_ref,
        gather_ref,
        slots_ref,
        slots_t_ref,
        window_ref,
        window_t_ref,
        row_bias_ref,
        level_bias_ref,
    )
    fetches = [
        pltpu.make_async_copy(outside[i], inside[i], fetch_sem.at[i]) for i in range(len(inside))
    ]
    for i in (0, 5, 1, 2, 3, 4, 6, 8, 10, 11, 7, 9):
        fetches[i].start()
    pl.semaphore_wait(barrier, len(greeted))

    def part_rows(w, core_side, third):
        tall = weights[w].shape[1] // PARTS
        return pl.ds(pl.multiple_of((core_side * 3 + third) * tall, tall), tall)

    def third_of(piece):
        return z_side if piece == 0 else 2

    def remote(src, dst, send, recv, to_lat, to_lon):
        return pltpu.make_async_remote_copy(
            src_ref=src,
            dst_ref=dst,
            send_sem=send,
            recv_sem=recv,
            device_id={"lat": to_lat, "lon": to_lon},
            device_id_type=MESH,
        )

    def lat_copy(w, k, piece):
        hop = hop_of(k, piece)
        origin = swapped(lat, k ^ hop)
        rows = part_rows(w, core, third_of(piece))
        dst = weights[w].at[origin, rows]
        src = sources[w].at[rows] if k == hop else dst
        return remote(
            src, dst, lat_send.at[w, k, piece], lat_recv.at[w, k, piece], swapped(lat, hop), lon
        )

    def z_copy(w, k):
        block = weights[w].at[swapped(lat, k), part_rows(w, core, z_side)]
        return remote(block, block, z_send.at[w, k], z_recv.at[w, k], lat, z_peer)

    def core_copy(w, k, place):
        third = (z_side, 2, 1 - z_side)[place]
        block = weights[w].at[swapped(lat, k), part_rows(w, core, third)]
        return remote(
            block, block, core_send.at[w, k, place], core_recv.at[w, k, place], lat, core_peer
        )

    def start_own(w):
        for step in range(2):
            for at, b in enumerate(bits):
                lat_copy(w, b, (step + at) % 2).start()

    arrivals = [(k, piece) for k in others for piece in range(2)]
    arrivals.sort(key=lambda a: (bin(a[0]).count("1"), (bits.index(hop_of(*a)) + a[1]) % 2))
    firsts = [a for a in arrivals if a[0] in bits]
    rest = [a for a in arrivals if a[0] not in bits]

    def pump(w, which):
        for k, piece in which:
            lat_copy(w, k, piece).wait_recv()
            for further in others:
                if further != k and further ^ hop_of(further, piece) == k:
                    lat_copy(w, further, piece).start()
            if piece == 0:
                z_copy(w, k).start()
            core_copy(w, k, piece).start()

    def pump_z(w):
        for k in others:
            z_copy(w, k).wait_recv()
            core_copy(w, k, 2).start()

    def finish(w):
        for k in others:
            for place in range(3):
                core_copy(w, k, place).wait_recv()

    def own_copy(w):
        return pltpu.make_async_copy(sources[w], weights[w].at[lat], own_sem.at[w])

    start_own(0)
    for w in range(3):
        own_copy(w).start()

    per_level = patches.shape[1] // levels
    width = x_ref.shape[2]
    fetches[0].wait()
    fetches[5].wait()
    for level in range(levels):
        moved = dot(gather_ref[...], x_ref[level])
        for ij in range(4):
            for at in range(0, width, 128):
                patches[
                    (ij * width + at) // 128, pl.ds(level, per_level, stride=levels), :
                ] = moved[ij * per_level : (ij + 1) * per_level, at : at + 128]
    pump(0, firsts)
    start_own(1)
    fetches[1].wait()
    fetches[2].wait()
    whole = jnp.concatenate([patches[b] for b in range(patches.shape[0])], axis=1)
    patch_normed[...] = normalize(whole, mg_ref[...][None], mb_ref[...][None]).astype(
        jnp.bfloat16
    )
    pump(0, rest)
    for i in (3, 4, 6, 7, 8, 9, 10, 11):
        fetches[i].wait()
    last = jnp.where(lat == lat_count - 1, 1.0, 0.0)
    bias[0] = row_bias_ref[...] * last
    bias[1] = jnp.minimum(row_bias_ref[...] * last, level_bias_ref[...])
    pump_z(0)
    start_own(2)
    for w in range(3):
        own_copy(w).wait()
    finish(0)

    def project(left_value, weight, store):
        count, rows, cols = weight.shape
        step = 256

        def one(i, carry):
            at = pl.ds(pl.multiple_of(i * step, step), step)
            store(at, dot(left_value, weight[:, :, at].reshape(count * rows, step)))
            return carry

        lax.fori_loop(0, cols // step, one, 0)

    def store_coarse(at, value):
        coarse[:, at] = value.astype(jnp.bfloat16)

    project(patch_normed[...], wm, store_coarse)

    pump(1, firsts)
    normed = normalize(coarse[...].astype(jnp.float32), cg_ref[...][None], cb_ref[...][None])
    own_slots[...] = dot(slots_ref[...], normed.astype(jnp.bfloat16)).astype(jnp.bfloat16)

    model = context.shape[1]
    split = model // BACK_PARTS

    def halo_copy(q):
        rows = pl.ds(q * padded, padded)
        to_lat, to_lon = ((lat, left), (up, lon), (up, left))[q - 1]
        return remote(
            own_slots.at[rows], frame.at[rows], halo_send.at[q], halo_recv.at[q], to_lat, to_lon
        )

    def back_copy(q, half):
        rows, lanes = pl.ds(q * padded, padded), pl.ds(half * split, split)
        to_lat, to_lon = ((lat, right), (down, lon), (down, right))[q - 1]
        return remote(
            back_slots.at[rows, lanes],
            home.at[rows, lanes],
            back_send.at[q, half],
            back_recv.at[q, half],
            to_lat,
            to_lon,
        )

    for q in (3, 2, 1):
        halo_copy(q).start()
    frame[pl.ds(0, padded)] = own_slots[pl.ds(0, padded)]
    pump(1, rest)
    pump_z(1)
    for q in (1, 2, 3):
        halo_copy(q).wait_recv()
    framed[...] = dot(window_ref[...], frame[...]).astype(jnp.bfloat16)
    finish(1)

    def store_projected(at, value):
        projected[:, at] = value.astype(jnp.bfloat16)

    project(framed[...], wq, store_projected)
    pump(2, firsts)

    depth = model // HEADS2
    packed = 128 // depth
    window = bias.shape[1]
    scale = depth ** (-0.5)
    lane = lax.broadcasted_iota(jnp.int32, (window, 128), 1)
    masks = [(lane >= h * depth) & (lane < (h + 1) * depth) for h in range(packed)]

    for half in range(BACK_PARTS):
        for g in range(levels // 2):
            rows = pl.ds(g * window, window)

            def one_group(i, carry):
                def lanes(which):
                    return pl.ds(pl.multiple_of(which * model + i * 128, 128), 128)

                queries = projected[rows, lanes(0)]
                keys = projected[rows, lanes(1)]
                values = projected[rows, lanes(2)]
                nothing = jnp.zeros_like(queries)
                stacked = jnp.concatenate([jnp.where(m, queries, nothing) for m in masks], axis=0)
                scores = lax.dot_general(
                    keys, stacked, (((1,), (1,)), ((), ())), preferred_element_type=jnp.float32
                )
                scores = scores * scale + bias[g]
                peak = jnp.max(scores, axis=0, keepdims=True)
                shares = jnp.exp(scores - peak)
                total = jnp.sum(shares, axis=0, keepdims=True)
                probs = (shares * (1.0 / total)).astype(jnp.bfloat16)
                mixed = lax.dot_general(
                    probs, values, (((0,), (0,)), ((), ())), preferred_element_type=jnp.float32
                )
                result = mixed[:window]
                for h in range(1, packed):
                    result = jnp.where(masks[h], mixed[h * window : (h + 1) * window], result)
                at = pl.ds(pl.multiple_of(i * 128, 128), 128)
                context[rows, at] = result.astype(jnp.bfloat16)
                return carry

            lax.fori_loop(half * split // 128, (half + 1) * split // 128, one_group, 0)
        lanes_of = pl.ds(half * split, split)
        back_slots[:, lanes_of] = dot(window_t_ref[...], context[:, lanes_of]).astype(jnp.bfloat16)
        for q in (3, 2, 1):
            back_copy(q, half).start()
        home[pl.ds(0, padded), lanes_of] = back_slots[pl.ds(0, padded), lanes_of]
        if half == 0:
            pump(2, rest)
            pump_z(2)
    finish(2)
    for q in (1, 2, 3):
        for half in range(BACK_PARTS):
            back_copy(q, half).wait_recv()
    ordered = dot(slots_t_ref[...], home[...]).astype(jnp.bfloat16)

    def store_out(at, value):
        out_ref[:, at] = (coarse[:, at].astype(jnp.float32) + value).astype(jnp.bfloat16)

    project(ordered, wo, store_out)

    for w in range(3):
        for k in others:
            for piece in range(2):
                lat_copy(w, k, piece).wait_send()
            z_copy(w, k).wait_send()
            for place in range(3):
                core_copy(w, k, place).wait_send()
    for q in (1, 2, 3):
        halo_copy(q).wait_send()
        for half in range(BACK_PARTS):
            back_copy(q, half).wait_send()


def shards(
    fine_input,
    merge_gain,
    merge_bias,
    merge_weight,
    coarse_gain,
    coarse_bias,
    coarse_qkv,
    coarse_out,
):
    lat_count, lon_count = lax.axis_size("lat"), lax.axis_size("lon")
    levels, fine_rows, fine_cols, width = fine_input.shape
    rows, cols = fine_rows // 2, fine_cols // 2
    model = merge_weight.shape[1]
    assert rows == 6 and cols == 12 and levels == 4
    assert lat_count & (lat_count - 1) == 0 and lon_count % 4 == 0
    gather, to_slots, to_window, row_bias, level_bias, padded = layout_tables(levels, rows, cols)
    tokens = levels * rows * cols
    half = jnp.bfloat16
    operands = (
        fine_input.reshape(levels, fine_rows * fine_cols, width),
        merge_gain,
        merge_bias,
        coarse_gain,
        coarse_bias,
        jnp.asarray(gather, half),
        jnp.asarray(to_slots, half),
        jnp.asarray(to_slots.T, half),
        jnp.asarray(to_window, half),
        jnp.asarray(to_window.T, half),
        jnp.asarray(row_bias),
        jnp.asarray(level_bias),
        merge_weight,
        coarse_qkv,
        coarse_out,
    )
    slots = SLOTS * padded
    window = tokens // (levels // 2)
    result = pl.pallas_call(
        functools.partial(body, (lat_count, lon_count, padded, levels)),
        out_shape=jax.ShapeDtypeStruct((tokens, model), half),
        in_specs=[pl.BlockSpec(memory_space=pl.ANY)] * len(operands),
        out_specs=pl.BlockSpec(memory_space=pltpu.VMEM),
        scratch_shapes=[
            pltpu.VMEM((lat_count,) + merge_weight.shape, half),
            pltpu.VMEM((lat_count,) + coarse_qkv.shape, half),
            pltpu.VMEM((lat_count,) + coarse_out.shape, half),
            pltpu.VMEM((4 * width // 128, tokens, 128), jnp.float32),
            pltpu.VMEM((tokens, 4 * width), half),
            pltpu.VMEM((tokens, model), half),
            pltpu.VMEM((slots, model), half),
            pltpu.VMEM((slots, model), half),
            pltpu.VMEM((tokens, model), half),
            pltpu.VMEM((tokens, 3 * model), half),
            pltpu.VMEM((tokens, model), half),
            pltpu.VMEM((slots, model), half),
            pltpu.VMEM((slots, model), half),
            pltpu.VMEM((2, window, 4 * window), jnp.float32),
            pltpu.SemaphoreType.DMA((3,)),
            pltpu.SemaphoreType.DMA((3, lat_count, 2)),
            pltpu.SemaphoreType.DMA((3, lat_count, 2)),
            pltpu.SemaphoreType.DMA((3, lat_count)),
            pltpu.SemaphoreType.DMA((3, lat_count)),
            pltpu.SemaphoreType.DMA((3, lat_count, 3)),
            pltpu.SemaphoreType.DMA((3, lat_count, 3)),
            pltpu.SemaphoreType.DMA((SLOTS,)),
            pltpu.SemaphoreType.DMA((SLOTS,)),
            pltpu.SemaphoreType.DMA((SLOTS, BACK_PARTS)),
            pltpu.SemaphoreType.DMA((SLOTS, BACK_PARTS)),
            pltpu.SemaphoreType.DMA((len(operands) - 3,)),
        ]
        + [pltpu.VMEM(operand.shape, operand.dtype) for operand in operands[:-3]],
        compiler_params=pltpu.CompilerParams(collective_id=0, has_side_effects=True),
    )(*operands)
    return result.reshape(rows, cols, levels, model).transpose(2, 0, 1, 3)


def solution(mesh):
    in_specs = (
        P(None, "lat", "lon", None),
        P(),
        P(),
        P("lat", None),
        P(),
        P(),
        P("lat", None),
        P("lat", None),
    )
    out_specs = P(None, "lat", "lon", None)
    return jax.shard_map(shards, mesh=mesh, in_specs=in_specs, out_specs=out_specs, check_vma=False)
```

```python
import functools

import jax
import jax.numpy as jnp
import numpy as np
from jax import lax
from jax.experimental import pallas as pl
from jax.experimental.pallas import tpu as pltpu
from jax.sharding import PartitionSpec as P

HEADS2 = 24
EPSILON = 1e-05
MESH = pl.DeviceIdType.MESH
BLOCKED = -1e30
SLOTS = 4
BACK_PARTS = 3
PARTS = 6


def swapped(index, bits):
    bit = 1
    while bit <= bits:
        if bits & bit:
            index = index + bit - 2 * bit * ((index // bit) % 2)
        bit *= 2
    return index


def low_bit(k):
    return k & -k


def high_bit(k):
    return 1 << (k.bit_length() - 1)


def hop_of(k, piece):
    return high_bit(k) if piece == 0 else low_bit(k)


def layout_tables(levels, rows, cols):
    half_rows, half_cols = rows // 2, cols // 2
    per_level = rows * cols
    tokens = levels * per_level
    per_slot = tokens // SLOTS
    padded = -(-per_slot // 16) * 16
    gather = np.zeros((4 * per_level, 4 * per_level), np.float32)
    for i in range(2):
        for j in range(2):
            for a in range(rows):
                for b in range(cols):
                    out_row = (2 * i + j) * per_level + a * cols + b
                    gather[out_row, (2 * a + i) * 2 * cols + 2 * b + j] = 1
    to_slots = np.zeros((SLOTS * padded, tokens), np.float32)
    to_window = np.zeros((tokens, SLOTS * padded), np.float32)
    groups = levels // 2
    window = tokens // groups
    part = window // SLOTS
    per_quarter = half_rows * half_cols
    for q in range(SLOTS):
        row_half, col_half = ((1, 1), (1, 0), (0, 1), (0, 0))[q]
        for f in range(levels):
            level = (f + 1) % levels
            for a in range(half_rows):
                for b in range(half_cols):
                    place = q * padded + (f * half_rows + a) * half_cols + b
                    natural = (row_half * half_rows + a) * cols + col_half * half_cols + b
                    to_slots[place, natural * levels + level] = 1
                    target = (f // 2) * window + q * part + (f % 2) * per_quarter
                    to_window[target + a * half_cols + b, place] = 1
    t = np.arange(window)
    row_id = t // (window // 2)
    level_id = (t // per_quarter) % 2
    row_bias = np.where(row_id[:, None] == row_id[None, :], 0.0, BLOCKED)
    level_bias = np.where(level_id[:, None] == level_id[None, :], 0.0, BLOCKED)
    return (
        gather,
        to_slots,
        to_window,
        np.tile(row_bias, (1, 4)).astype(np.float32),
        np.tile(level_bias, (1, 4)).astype(np.float32),
        padded,
    )


def normalize(values, norm_gain, norm_bias):
    average = jnp.mean(values, axis=-1, keepdims=True)
    centered = values - average
    spread = jnp.mean(centered * centered, axis=-1, keepdims=True)
    return centered * lax.rsqrt(spread + EPSILON) * norm_gain + norm_bias


def dot(a, b):
    return jnp.dot(a, b, preferred_element_type=jnp.float32)


def body(
    dims,
    x_in,
    mg_in,
    mb_in,
    cg_in,
    cb_in,
    gather_in,
    slots_in,
    slots_t_in,
    window_in,
    window_t_in,
    row_bias_in,
    level_bias_in,
    wm_in,
    wq_in,
    wo_in,
    out_ref,
    wm,
    wq,
    wo,
    patches,
    patch_normed,
    coarse,
    own_slots,
    frame,
    framed,
    projected,
    context,
    back_slots,
    home,
    bias,
    own_sem,
    lat_send,
    lat_recv,
    z_send,
    z_recv,
    core_send,
    core_recv,
    halo_send,
    halo_recv,
    back_send,
    back_recv,
    fetch_sem,
    x_ref,
    mg_ref,
    mb_ref,
    cg_ref,
    cb_ref,
    gather_ref,
    slots_ref,
    slots_t_ref,
    window_ref,
    window_t_ref,
    row_bias_ref,
    level_bias_ref,
):
    lat_count, lon_count, padded, levels = dims
    lat, lon = lax.axis_index("lat"), lax.axis_index("lon")
    core = lon % 2
    z_side = (lon // 2) % 2
    sources, weights = (wm_in, wq_in, wo_in), (wm, wq, wo)
    bits = [1 << b for b in range(lat_count.bit_length() - 1)]
    others = sorted(range(1, lat_count), key=lambda k: (bin(k).count("1"), k))
    up, down = (lat + lat_count - 1) % lat_count, (lat + 1) % lat_count
    left, right = (lon + lon_count - 1) % lon_count, (lon + 1) % lon_count
    z_peer, core_peer = swapped(lon, 2), swapped(lon, 1)

    barrier = pltpu.get_barrier_semaphore()
    greeted = [(swapped(lat, b), lon) for b in bits]
    greeted += [(lat, z_peer), (lat, core_peer)]
    greeted += [(up, lon), (down, lon), (lat, left), (lat, right), (up, left), (down, right)]
    for to_lat, to_lon in greeted:
        pl.semaphore_signal(
            barrier, inc=1, device_id={"lat": to_lat, "lon": to_lon}, device_id_type=MESH
        )
    outside = (
        x_in,
        mg_in,
        mb_in,
        cg_in,
        cb_in,
        gather_in,
        slots_in,
        slots_t_in,
        window_in,
        window_t_in,
        row_bias_in,
        level_bias_in,
    )
    inside = (
        x_ref,
        mg_ref,
        mb_ref,
        cg_ref,
        cb_ref,
        gather_ref,
        slots_ref,
        slots_t_ref,
        window_ref,
        window_t_ref,
        row_bias_ref,
        level_bias_ref,
    )
    fetches = [
        pltpu.make_async_copy(outside[i], inside[i], fetch_sem.at[i]) for i in range(len(inside))
    ]
    for i in (0, 5, 1, 2, 3, 4, 6, 8, 10, 11, 7, 9):
        fetches[i].start()
    pl.semaphore_wait(barrier, len(greeted))

    def part_rows(w, core_side, third):
        tall = weights[w].shape[1] // PARTS
        return pl.ds(pl.multiple_of((core_side * 3 + third) * tall, tall), tall)

    def third_of(piece):
        return z_side if piece == 0 else 2

    def remote(src, dst, send, recv, to_lat, to_lon):
        return pltpu.make_async_remote_copy(
            src_ref=src,
            dst_ref=dst,
            send_sem=send,
            recv_sem=recv,
            device_id={"lat": to_lat, "lon": to_lon},
            device_id_type=MESH,
        )

    def lat_copy(w, k, piece):
        hop = hop_of(k, piece)
        origin = swapped(lat, k ^ hop)
        rows = part_rows(w, core, third_of(piece))
        dst = weights[w].at[origin, rows]
        src = sources[w].at[rows] if k == hop else dst
        return remote(
            src, dst, lat_send.at[w, k, piece], lat_recv.at[w, k, piece], swapped(lat, hop), lon
        )

    def z_copy(w, k):
        block = weights[w].at[swapped(lat, k), part_rows(w, core, z_side)]
        return remote(block, block, z_send.at[w, k], z_recv.at[w, k], lat, z_peer)

    def core_copy(w, k, place):
        third = (z_side, 2, 1 - z_side)[place]
        block = weights[w].at[swapped(lat, k), part_rows(w, core, third)]
        return remote(
            block, block, core_send.at[w, k, place], core_recv.at[w, k, place], lat, core_peer
        )

    def start_own(w):
        for step in range(2):
            for at, b in enumerate(bits):
                lat_copy(w, b, (step + at) % 2).start()

    arrivals = [(k, piece) for k in others for piece in range(2)]
    arrivals.sort(key=lambda a: (bin(a[0]).count("1"), (bits.index(hop_of(*a)) + a[1]) % 2))
    firsts = [a for a in arrivals if a[0] in bits]
    rest = [a for a in arrivals if a[0] not in bits]

    def pump(w, which):
        for k, piece in which:
            lat_copy(w, k, piece).wait_recv()
            for further in others:
                if further != k and further ^ hop_of(further, piece) == k:
                    lat_copy(w, further, piece).start()
            if piece == 0:
                z_copy(w, k).start()
            core_copy(w, k, piece).start()

    def pump_z(w):
        for k in others:
            z_copy(w, k).wait_recv()
            core_copy(w, k, 2).start()

    def finish(w):
        for k in others:
            for place in range(3):
                core_copy(w, k, place).wait_recv()

    def own_copy(w):
        return pltpu.make_async_copy(sources[w], weights[w].at[lat], own_sem.at[w])

    start_own(0)
    for w in range(3):
        own_copy(w).start()

    per_level = patches.shape[1] // levels
    width = x_ref.shape[2]
    fetches[0].wait()
    fetches[5].wait()
    for level in range(levels):
        moved = dot(gather_ref[...], x_ref[level])
        for ij in range(4):
            for at in range(0, width, 128):
                patches[
                    (ij * width + at) // 128, pl.ds(level, per_level, stride=levels), :
                ] = moved[ij * per_level : (ij + 1) * per_level, at : at + 128]
    pump(0, firsts)
    start_own(1)
    fetches[1].wait()
    fetches[2].wait()
    whole = jnp.concatenate([patches[b] for b in range(patches.shape[0])], axis=1)
    patch_normed[...] = normalize(whole, mg_ref[...][None], mb_ref[...][None]).astype(
        jnp.bfloat16
    )
    pump(0, rest)
    for i in (3, 4, 6, 7, 8, 9, 10, 11):
        fetches[i].wait()
    last = jnp.where(lat == lat_count - 1, 1.0, 0.0)
    bias[0] = row_bias_ref[...] * last
    bias[1] = jnp.minimum(row_bias_ref[...] * last, level_bias_ref[...])
    pump_z(0)
    start_own(2)
    for w in range(3):
        own_copy(w).wait()
    finish(0)

    def project(left_value, weight, store):
        count, rows, cols = weight.shape
        step = 256

        def one(i, carry):
            at = pl.ds(pl.multiple_of(i * step, step), step)
            store(at, dot(left_value, weight[:, :, at].reshape(count * rows, step)))
            return carry

        lax.fori_loop(0, cols // step, one, 0)

    def store_coarse(at, value):
        coarse[:, at] = value.astype(jnp.bfloat16)

    project(patch_normed[...], wm, store_coarse)

    pump(1, firsts)
    normed = normalize(coarse[...].astype(jnp.float32), cg_ref[...][None], cb_ref[...][None])
    own_slots[...] = dot(slots_ref[...], normed.astype(jnp.bfloat16)).astype(jnp.bfloat16)

    model = context.shape[1]
    split = model // BACK_PARTS

    def halo_copy(q):
        rows = pl.ds(q * padded, padded)
        to_lat, to_lon = ((lat, left), (up, lon), (up, left))[q - 1]
        return remote(
            own_slots.at[rows], frame.at[rows], halo_send.at[q], halo_recv.at[q], to_lat, to_lon
        )

    def back_copy(q, half):
        rows, lanes = pl.ds(q * padded, padded), pl.ds(half * split, split)
        to_lat, to_lon = ((lat, right), (down, lon), (down, right))[q - 1]
        return remote(
            back_slots.at[rows, lanes],
            home.at[rows, lanes],
            back_send.at[q, half],
            back_recv.at[q, half],
            to_lat,
            to_lon,
        )

    for q in (3, 2, 1):
        halo_copy(q).start()
    frame[pl.ds(0, padded)] = own_slots[pl.ds(0, padded)]
    pump(1, rest)
    pump_z(1)
    for q in (1, 2, 3):
        halo_copy(q).wait_recv()
    framed[...] = dot(window_ref[...], frame[...]).astype(jnp.bfloat16)
    finish(1)

    def store_projected(at, value):
        projected[:, at] = value.astype(jnp.bfloat16)

    project(framed[...], wq, store_projected)
    pump(2, firsts)

    depth = model // HEADS2
    packed = 128 // depth
    window = bias.shape[1]
    scale = depth ** (-0.5)
    lane = lax.broadcasted_iota(jnp.int32, (window, 128), 1)
    masks = [(lane >= h * depth) & (lane < (h + 1) * depth) for h in range(packed)]

    for half in range(BACK_PARTS):
        for g in range(levels // 2):
            rows = pl.ds(g * window, window)

            def one_group(i, carry):
                def lanes(which):
                    return pl.ds(pl.multiple_of(which * model + i * 128, 128), 128)

                queries = projected[rows, lanes(0)]
                keys = projected[rows, lanes(1)]
                values = projected[rows, lanes(2)]
                nothing = jnp.zeros_like(queries)
                stacked = jnp.concatenate([jnp.where(m, queries, nothing) for m in masks], axis=0)
                scores = lax.dot_general(
                    keys, stacked, (((1,), (1,)), ((), ())), preferred_element_type=jnp.float32
                )
                scores = scores * scale + bias[g]
                peak = jnp.max(scores, axis=0, keepdims=True)
                shares = jnp.exp(scores - peak)
                total = jnp.sum(shares, axis=0, keepdims=True)
                probs = (shares * (1.0 / total)).astype(jnp.bfloat16)
                mixed = lax.dot_general(
                    probs, values, (((0,), (0,)), ((), ())), preferred_element_type=jnp.float32
                )
                result = mixed[:window]
                for h in range(1, packed):
                    result = jnp.where(masks[h], mixed[h * window : (h + 1) * window], result)
                at = pl.ds(pl.multiple_of(i * 128, 128), 128)
                context[rows, at] = result.astype(jnp.bfloat16)
                return carry

            lax.fori_loop(half * split // 128, (half + 1) * split // 128, one_group, 0)
        lanes_of = pl.ds(half * split, split)
        back_slots[:, lanes_of] = dot(window_t_ref[...], context[:, lanes_of]).astype(jnp.bfloat16)
        for q in (3, 2, 1):
            back_copy(q, half).start()
        home[pl.ds(0, padded), lanes_of] = back_slots[pl.ds(0, padded), lanes_of]
        if half == 0:
            pump(2, rest)
            pump_z(2)
    finish(2)
    for q in (1, 2, 3):
        for half in range(BACK_PARTS):
            back_copy(q, half).wait_recv()
    ordered = dot(slots_t_ref[...], home[...]).astype(jnp.bfloat16)

    def store_out(at, value):
        total = coarse[:, at].astype(jnp.float32) + value
        out_ref[:, :, at] = total.reshape(-1, levels, total.shape[1]).astype(jnp.bfloat16)

    project(ordered, wo, store_out)

    for w in range(3):
        for k in others:
            for piece in range(2):
                lat_copy(w, k, piece).wait_send()
            z_copy(w, k).wait_send()
            for place in range(3):
                core_copy(w, k, place).wait_send()
    for q in (1, 2, 3):
        halo_copy(q).wait_send()
        for half in range(BACK_PARTS):
            back_copy(q, half).wait_send()


def shards(
    fine_input,
    merge_gain,
    merge_bias,
    merge_weight,
    coarse_gain,
    coarse_bias,
    coarse_qkv,
    coarse_out,
):
    lat_count, lon_count = lax.axis_size("lat"), lax.axis_size("lon")
    levels, fine_rows, fine_cols, width = fine_input.shape
    rows, cols = fine_rows // 2, fine_cols // 2
    model = merge_weight.shape[1]
    assert rows == 6 and cols == 12 and levels == 4
    assert lat_count & (lat_count - 1) == 0 and lon_count % 4 == 0
    gather, to_slots, to_window, row_bias, level_bias, padded = layout_tables(levels, rows, cols)
    tokens = levels * rows * cols
    half = jnp.bfloat16
    operands = (
        fine_input.reshape(levels, fine_rows * fine_cols, width),
        merge_gain,
        merge_bias,
        coarse_gain,
        coarse_bias,
        jnp.asarray(gather, half),
        jnp.asarray(to_slots, half),
        jnp.asarray(to_slots.T, half),
        jnp.asarray(to_window, half),
        jnp.asarray(to_window.T, half),
        jnp.asarray(row_bias),
        jnp.asarray(level_bias),
        merge_weight,
        coarse_qkv,
        coarse_out,
    )
    slots = SLOTS * padded
    window = tokens // (levels // 2)
    result = pl.pallas_call(
        functools.partial(body, (lat_count, lon_count, padded, levels)),
        out_shape=jax.ShapeDtypeStruct((rows * cols, levels, model), half),
        in_specs=[pl.BlockSpec(memory_space=pl.ANY)] * len(operands),
        out_specs=pl.BlockSpec(memory_space=pltpu.VMEM),
        scratch_shapes=[
            pltpu.VMEM((lat_count,) + merge_weight.shape, half),
            pltpu.VMEM((lat_count,) + coarse_qkv.shape, half),
            pltpu.VMEM((lat_count,) + coarse_out.shape, half),
            pltpu.VMEM((4 * width // 128, tokens, 128), jnp.float32),
            pltpu.VMEM((tokens, 4 * width), half),
            pltpu.VMEM((tokens, model), half),
            pltpu.VMEM((slots, model), half),
            pltpu.VMEM((slots, model), half),
            pltpu.VMEM((tokens, model), half),
            pltpu.VMEM((tokens, 3 * model), half),
            pltpu.VMEM((tokens, model), half),
            pltpu.VMEM((slots, model), half),
            pltpu.VMEM((slots, model), half),
            pltpu.VMEM((2, window, 4 * window), jnp.float32),
            pltpu.SemaphoreType.DMA((3,)),
            pltpu.SemaphoreType.DMA((3, lat_count, 2)),
            pltpu.SemaphoreType.DMA((3, lat_count, 2)),
            pltpu.SemaphoreType.DMA((3, lat_count)),
            pltpu.SemaphoreType.DMA((3, lat_count)),
            pltpu.SemaphoreType.DMA((3, lat_count, 3)),
            pltpu.SemaphoreType.DMA((3, lat_count, 3)),
            pltpu.SemaphoreType.DMA((SLOTS,)),
            pltpu.SemaphoreType.DMA((SLOTS,)),
            pltpu.SemaphoreType.DMA((SLOTS, BACK_PARTS)),
            pltpu.SemaphoreType.DMA((SLOTS, BACK_PARTS)),
            pltpu.SemaphoreType.DMA((len(operands) - 3,)),
        ]
        + [pltpu.VMEM(operand.shape, operand.dtype) for operand in operands[:-3]],
        compiler_params=pltpu.CompilerParams(collective_id=0, has_side_effects=True),
    )(*operands)
    return result.reshape(rows, cols, levels, model).transpose(2, 0, 1, 3)


def solution(mesh):
    in_specs = (
        P(None, "lat", "lon", None),
        P(),
        P(),
        P("lat", None),
        P(),
        P(),
        P("lat", None),
        P("lat", None),
    )
    out_specs = P(None, "lat", "lon", None)
    return jax.shard_map(shards, mesh=mesh, in_specs=in_specs, out_specs=out_specs, check_vma=False)
```
